128 devices in a mesh: gx: 16 (over z_lo, x, core), gy: 8 (over z_hi, y).
Axes of the slice: x: 4, y: 4, z: 4 (z_hi: 2, z_lo: 2; z = z_hi * 2 + z_lo), core: 2. Of those that a mesh axis runs over, the one named last changes fastest.
Arguments:
- scalar: float32 [1024, 512, 512], P('gx', 'gy'), may hold values from -6 to 6
- prefactor: float32 [1024, 512, 512], P('gx', 'gy'), may hold values from 0.05 to 1
- factor_x: float32 [1024, 512], P('gx'), may hold values from -0.25 to 0.25
- factor_y: float32 [512, 64], P('gy'), may hold values from -0.375 to 0.375
- factor_z: bfloat16 [512, 128], replicated, may hold values from -0.25 to 0.25
Outputs:
- advanced: float32 [1024, 512, 512], P('gx', 'gy')
- core: float32 [512, 64, 128], P('gx', 'gy')
The draws below stay inside these ranges and needn't reach their ends.
All inputs are finite; a program needn't handle non-finite values.
Results may differ from the reference program's by a relative error of at most 0.0029.
Values sent between devices are 32-bit elements; how exact they have to be, the bound alone decides.
A program may use at most 128 MiB of HBM per device.

```python
import math
import jax
import jax.numpy as jnp
from jax import lax

NZ = 512
RX = 512
RY = 64
RZ = 128
NX = 1024
NY = 512


def raised(entries, key, source, target, parts, factor):
    def block_of(axis_at):
        return (jnp.arange(entries.shape[axis_at]) // (entries.shape[axis_at] // parts)).reshape((-1,) + (1,) * (entries.ndim - 1 - axis_at))

    near = jax.random.permutation(key, parts)[block_of(target)]
    other_side = (block_of(target) + parts // 2) % parts
    return jnp.where((block_of(source) == near) | (block_of(source) == other_side), factor * entries, entries)


def steps_of(rng, dims, cuts, smallest, top_value):
    def one(axis_at, blocks):
        steps = jax.random.uniform(jax.random.fold_in(jax.random.fold_in(rng, 6), axis_at), (blocks,), jnp.float32, smallest / len(cuts), top_value / len(cuts))
        return jnp.repeat(jnp.exp(steps), dims[axis_at] // blocks).reshape((-1,) + (1,) * (len(dims) - axis_at - 1))

    gain = one(*cuts[0])
    for cut in cuts[1:]:
        gain = gain * one(*cut)
    return gain


def normal_values(key, extent, scale, limit, pieces=(), kind=jnp.bfloat16):
    factor_of = steps_of(key, extent, pieces, -0.22, 0.18) if pieces else 1.0
    entries = jax.random.normal(key, extent, jnp.float32) * scale * factor_of
    return jnp.minimum(jnp.maximum(entries, -limit), limit).astype(kind)


def bell_draw_with(own_key, extent, deviation, reach, shards, heavy, kind=jnp.bfloat16):
    entries = deviation * jax.random.normal(own_key, extent, jnp.float32)
    if shards:
        entries = entries * steps_of(own_key, extent, shards, -0.22, 0.18)
    return jnp.clip(raised(entries, jax.random.fold_in(own_key, 3), *heavy), -reach, reach).astype(kind)


def setup_inputs(seed: int = 0) -> dict:
    splits = jax.random.split(jax.random.key(seed), 6)
    scalar = normal_values(splits[0], (NX, NY, NZ), 1.0, 6.0, ((0, 16), (1, 8)), jnp.float32)
    prefactor = jnp.clip(jnp.exp(math.log(1.0) - 2.9957323 * jax.random.uniform(splits[1], (NX, NY, NZ), jnp.float32) ** steps_of(splits[1], (NX, NY, NZ), ((0, 16), (1, 8)), -0.2, 0.2)), 0.05, 1.0)
    factor_x = bell_draw_with(splits[2], (NX, RX), NX ** -0.5, 0.25, ((0, 16),), (0, 1, 16, 2.0), jnp.float32)
    factor_y = bell_draw_with(splits[3], (NY, RY), NY ** -0.5, 0.375, ((0, 8),), (0, 1, 8, 2.0), jnp.float32)
    factor_z = normal_values(splits[4], (NZ, RZ), NZ ** -0.5, 0.25)
    return dict(scalar=scalar, prefactor=prefactor, factor_x=factor_x, factor_y=factor_y, factor_z=factor_z)


spread_rate = 0.12
activation = 2.0


def laplace(padded):
    center = padded[1:-1, 1:-1]
    z_padded = jnp.pad(center, ((0, 0), (0, 0), (1, 1)))
    beside = padded[2:, 1:-1] + padded[:-2, 1:-1] + padded[1:-1, 2:] + padded[1:-1, :-2]
    beside = beside + z_padded[:, :, 2:] + z_padded[:, :, :-2]
    return beside - 6.0 * center


def sources(field, prefactor):
    return prefactor * jnp.exp(-activation / (1.0 + field * field))


def rate(field, prefactor):
    padded = jnp.pad(field, ((1, 1), (1, 1), (0, 0)))
    return spread_rate * laplace(padded) + sources(field, prefactor)


def reference(scalar, prefactor, factor_x, factor_y, factor_z):
    first = rate(scalar, prefactor)
    middle = scalar + first
    second = rate(middle, prefactor)
    advanced = scalar + 0.5 * (first + second)
    lowered = lax.optimization_barrier(advanced.astype(jnp.bfloat16)).astype(jnp.float32)
    z_reduced = jnp.dot(lowered.reshape(NX * NY, NZ), factor_z.astype(jnp.float32),
                        precision=lax.Precision.HIGHEST).reshape(NX, NY, RZ)
    y_reduced = jnp.einsum("xyc,yb->xbc", z_reduced, factor_y, precision=lax.Precision.HIGHEST)
    core = jnp.einsum("xa,xbc->abc", factor_x, y_reduced, precision=lax.Precision.HIGHEST)
    return advanced, core
```

```python
import jax
import jax.numpy as jnp
from jax import lax
from jax.experimental import pallas as pl
from jax.experimental.pallas import tpu as pltpu
from jax.sharding import PartitionSpec as P

MESH = pl.DeviceIdType.MESH
spread_rate = 0.12
activation = 2.0
PLANES, ROWS, LANES, PARTS = 64, 64, 128, 4
CHUNK = 8
CHUNKS = PLANES // CHUNK
TOP = 8
BAND = 16


def split(value):
    high = value.astype(jnp.bfloat16)
    low = (value - high.astype(jnp.float32)).astype(jnp.bfloat16)
    return high, low


def kernel(
    scalar, prefactor, factor_x, factor_y, factor_z, advanced, core_out,
    field, middle, pref, lowered, fz, fy, fx_all, fy_t, fx_t,
    faces_s, halo_s, faces_m, halo_m,
    y_red, y_in1, y_in2, z_in, gathered, x_out, x_in,
    load_sem, pref_sem, small_sem,
    fs_send, fs_recv, fm_send, fm_recv, xs_send, xs_recv, xm_send, xm_recv,
    fx_send, fx_recv, y1_send, y1_recv, y2_send, y2_recv, z_send, z_recv, c_send, c_recv, xr_send, xr_recv,
):
    gx, gy = lax.axis_index("gx"), lax.axis_index("gy")
    core, x, zl = gx % 2, (gx // 2) % 4, gx // 8
    y, zh = gy % 4, gy // 4

    def device(core, x, zl, y, zh):
        return (zl * 8 + x * 2 + core, zh * 4 + y)

    up_x, down_x = ((gx + 1) % 16, gy), ((gx + 15) % 16, gy)
    up_y, down_y = (gx, (gy + 1) % 8), (gx, (gy + 7) % 8)
    y_by1 = y + 1 - 2 * (y % 2)
    y_by3 = 3 - y
    pair_a, pair_b = device(core, x, zl, y_by1, zh), device(core, x, zl, y_by3, zh)
    z_peers = [device(core, x, 1 - zl, y, zh), device(core, x, zl, y, 1 - zh), device(core, x, 1 - zl, y, 1 - zh)]
    partner = device(1 - core, x, zl, y, zh)
    fx_peers = [partner, z_peers[0], device(1 - core, x, 1 - zl, y, zh)]
    x_peers = [device(core, (x + j) % 4, zl, y, zh) for j in (1, 2, 3)]

    def load(k, part):
        return pltpu.make_async_copy(
            scalar.at[pl.ds(k * CHUNK, CHUNK), :, pl.ds(part * LANES, LANES)],
            field.at[pl.ds(k * CHUNK + 1, CHUNK), part, pl.ds(TOP, ROWS), :],
            load_sem.at[k, part],
        )

    def load_pref(k):
        rows = pl.ds(k * CHUNK, CHUNK)
        return pltpu.make_async_copy(prefactor.at[rows], pref.at[rows], pref_sem.at[k])

    for k in [7, 0, 6, 1, 2, 3, 4, 5]:
        for part in range(PARTS):
            load(k, part).start()
    fx_load = pltpu.make_async_copy(factor_x, fx_all.at[core, zl], small_sem.at[0])
    fz_load = pltpu.make_async_copy(factor_z, fz, small_sem.at[1])
    fy_load = pltpu.make_async_copy(factor_y, fy, small_sem.at[2])
    fx_load.start()
    for k in [7, 0, 1]:
        load_pref(k).start()
    fz_load.start()
    fy_load.start()
    for k in [2, 3, 4, 5, 6]:
        load_pref(k).start()

    barrier = pltpu.get_barrier_semaphore()
    peers = [up_x, down_x, up_y, down_y, pair_a, pair_b, *z_peers, partner, fx_peers[2], *x_peers]
    for peer in peers:
        pl.semaphore_signal(barrier, inc=1, device_id=peer, device_id_type=MESH)
    pl.semaphore_wait(barrier, len(peers))

    def remote(src, dst, send, recv, to):
        return pltpu.make_async_remote_copy(
            src_ref=src, dst_ref=dst, send_sem=send, recv_sem=recv, device_id=to, device_id_type=MESH
        )

    def plane_of(buffer, index):
        return buffer.at[index, :, pl.ds(TOP, ROWS), :]

    def x_faces(buffer, send, recv):
        low = remote(plane_of(buffer, 1), plane_of(buffer, PLANES + 1), send.at[0], recv.at[0], down_x)
        high = remote(plane_of(buffer, PLANES), plane_of(buffer, 0), send.at[1], recv.at[1], up_x)
        return low, high

    def y_faces(faces, halo, send, recv, k):
        rows = pl.ds(k * CHUNK * PARTS, CHUNK * PARTS)
        low = remote(faces.at[0, rows], halo.at[1, rows], send.at[0, k], recv.at[0, k], down_y)
        high = remote(faces.at[1, rows], halo.at[0, rows], send.at[1, k], recv.at[1, k], up_y)
        return low, high

    s_low, s_high = x_faces(field, xs_send, xs_recv)
    m_low, m_high = x_faces(middle, xm_send, xm_recv)

    def send_faces(k):
        for part in range(PARTS):
            load(k, part).wait()
        for i in range(CHUNK):
            for part in range(PARTS):
                at = pl.ds((k * CHUNK + i) * PARTS + part, 1)
                faces_s[0, at, :] = field[k * CHUNK + i + 1, part, TOP : TOP + 1, :]
                faces_s[1, at, :] = field[k * CHUNK + i + 1, part, TOP + ROWS - 1 : TOP + ROWS, :]
        for copy in y_faces(faces_s, halo_s, fs_send, fs_recv, k):
            copy.start()

    send_faces(7)
    s_high.start()
    send_faces(0)
    s_low.start()
    send_faces(6)

    def rest(k, carry):
        send_faces(k)
        return carry

    lax.fori_loop(1, 6, rest, 0)

    fx_copies = [
        remote(fx_all.at[core, zl], fx_all.at[core, zl], fx_send.at[i], fx_recv.at[i], to)
        for i, to in enumerate(fx_peers)
    ]
    fx_load.wait()
    for copy in fx_copies:
        copy.start()
    fz_load.wait()
    fy_load.wait()
    eye = (
        lax.broadcasted_iota(jnp.int32, (64, 64), 0) == lax.broadcasted_iota(jnp.int32, (64, 64), 1)
    ).astype(jnp.bfloat16)
    turned = (((1,), (1,)), ((), ()))
    fy_high, fy_low = (
        lax.dot_general(eye, part, turned, preferred_element_type=jnp.float32).astype(jnp.bfloat16)
        for part in split(fy[...])
    )
    fy_t[...] = jnp.concatenate([fy_high, fy_high, fy_low], axis=1)

    lane = lax.broadcasted_iota(jnp.int32, (BAND, LANES), 1)
    at_left, at_right = lane == 0, lane == LANES - 1

    def fill_halo(buffer, halo, plane):
        for part in range(PARTS):
            at = pl.ds(plane * PARTS + part, 1)
            buffer[plane + 1, part, TOP - 1 : TOP, :] = jnp.where(gy > 0, halo[0, at, :], 0.0)
            buffer[plane + 1, part, TOP + ROWS : TOP + ROWS + 1, :] = jnp.where(gy < 7, halo[1, at, :], 0.0)

    def stepped(buffer, plane, row):
        at = plane + 1
        own = slice(TOP + row, TOP + row + BAND)
        centers = [buffer[at, part, own, :] for part in range(PARTS)]
        lefts = [pltpu.roll(c, 1, 1) for c in centers]
        rights = [pltpu.roll(c, LANES - 1, 1) for c in centers]
        results = []
        for part, c in enumerate(centers):
            left = jnp.where(at_left, lefts[part - 1] if part > 0 else 0.0, lefts[part])
            right = jnp.where(at_right, rights[part + 1] if part + 1 < PARTS else 0.0, rights[part])
            beside = buffer[at + 1, part, own, :] + buffer[at - 1, part, own, :]
            beside = beside + (
                buffer[at, part, TOP + row + 1 : TOP + row + 1 + BAND, :]
                + buffer[at, part, TOP + row - 1 : TOP + row - 1 + BAND, :]
            )
            beside = beside + (left + right)
            factor = pref[plane, row : row + BAND, part * LANES : (part + 1) * LANES]
            source = factor * jnp.exp(-activation / (1.0 + c * c))
            results.append((1.0 - 6.0 * spread_rate) * c + spread_rate * beside + source)
        return results

    def clear_plane(buffer, index):
        for part in range(PARTS):
            buffer[index, part, TOP : TOP + ROWS, :] = jnp.zeros((ROWS, LANES), jnp.float32)

    def first_stage(k):
        load_pref(k).wait()
        low, high = y_faces(faces_s, halo_s, fs_send, fs_recv, k)
        low.wait_recv()
        high.wait_recv()

        @pl.when(k == CHUNKS - 1)
        def _():
            s_low.wait_recv()

            @pl.when(gx == 15)
            def _():
                clear_plane(field, PLANES + 1)

        @pl.when(k == 0)
        def _():
            s_high.wait_recv()

            @pl.when(gx == 0)
            def _():
                clear_plane(field, 0)

        def plane_step(i, carry):
            plane = k * CHUNK + i
            fill_halo(field, halo_s, plane)
            for row in range(0, ROWS, BAND):
                for part, value in enumerate(stepped(field, plane, row)):
                    middle[plane + 1, part, TOP + row : TOP + row + BAND, :] = value
                    at = pl.ds(plane * PARTS + part, 1)
                    if row == 0:
                        faces_m[0, at, :] = value[0:1, :]
                    if row == ROWS - BAND:
                        faces_m[1, at, :] = value[BAND - 1 : BAND, :]
            return carry

        lax.fori_loop(0, CHUNK, plane_step, 0)
        for copy in y_faces(faces_m, halo_m, fm_send, fm_recv, k):
            copy.start()

        @pl.when(k == CHUNKS - 1)
        def _():
            m_high.start()

        @pl.when(k == 0)
        def _():
            m_low.start()

    def y_first(k):
        a = remote(y_red.at[k, pl.ds(1, 2), :, pl.ds(0, 4)], y_in1.at[k, 0], y1_send.at[k, 0], y1_recv.at[k, 0], pair_a)
        b = remote(y_red.at[k, pl.ds(2, 2), :, pl.ds(4, 4)], y_in1.at[k, 1], y1_send.at[k, 1], y1_recv.at[k, 1], pair_b)
        return a, b

    def y_second(k):
        a = remote(y_red.at[k, 3, :, pl.ds(0, 4)], y_in2.at[k, 0], y2_send.at[k, 0], y2_recv.at[k, 0], pair_b)
        b = remote(y_red.at[k, 1, :, pl.ds(4, 4)], y_in2.at[k, 1], y2_send.at[k, 1], y2_recv.at[k, 1], pair_a)
        return a, b

    def z_copies(k):
        return [
            remote(y_red.at[k, 0, block], z_in.at[k, i], z_send.at[k, i], z_recv.at[k, i], z_peers[i])
            for i, block in enumerate((zh, 1 - zh, 1 - zh))
        ]

    def core_copy(k):
        block = gathered.at[core, :, pl.ds(k * CHUNK, CHUNK)]
        return remote(block, block, c_send.at[k], c_recv.at[k], partner)

    def second_stage(k):
        low, high = y_faces(faces_m, halo_m, fm_send, fm_recv, k)
        low.wait_recv()
        high.wait_recv()

        @pl.when(k == CHUNKS - 1)
        def _():
            m_low.wait_recv()

            @pl.when(gx == 15)
            def _():
                clear_plane(middle, PLANES + 1)

        @pl.when(k == 0)
        def _():
            m_high.wait_recv()

            @pl.when(gx == 0)
            def _():
                clear_plane(middle, 0)

        def plane_step(i, carry):
            plane = k * CHUNK + i
            fill_halo(middle, halo_m, plane)
            for row in range(0, ROWS, BAND):
                for part, value in enumerate(stepped(middle, plane, row)):
                    value = 0.5 * (field[plane + 1, part, TOP + row : TOP + row + BAND, :] + value)
                    lanes = slice(part * LANES, (part + 1) * LANES)
                    advanced[plane, row : row + BAND, lanes] = value
                    lowered[i, row : row + BAND, lanes] = value.astype(jnp.bfloat16)
            return carry

        lax.fori_loop(0, CHUNK, plane_step, 0)
        z_red = jnp.dot(
            lowered[...].reshape(CHUNK * ROWS, PARTS * LANES), fz[...], preferred_element_type=jnp.float32
        )
        blocks = [y, y_by1, (y + 2) % 4, y_by3]
        for i in range(0, CHUNK, 2):
            pair = jnp.concatenate([z_red[i * ROWS : (i + 1) * ROWS], z_red[(i + 1) * ROWS : (i + 2) * ROWS]], axis=1)
            high, low = split(pair)
            stacked = jnp.concatenate([high, low, high], axis=0)
            both = jnp.dot(fy_t[...], stacked, preferred_element_type=jnp.float32)
            for owner in range(8):
                for j in range(2):
                    y_red[k, blocks[owner % 4], owner // 4, i + j] = both[
                        owner * 8 : owner * 8 + 8, j * LANES : (j + 1) * LANES
                    ]
        for copy in y_first(k):
            copy.start()

    def y_first_done(k):
        for copy in y_first(k):
            copy.wait_recv()
        y_red[k, 0, :, 0:4] += y_in1[k, 0, 0]
        y_red[k, 3, :, 0:4] += y_in1[k, 0, 1]
        y_red[k, 1, :, 4:8] += y_in1[k, 1, 0]
        y_red[k, 0, :, 4:8] += y_in1[k, 1, 1]
        for copy in y_second(k):
            copy.start()

    def y_second_done(k):
        for copy in y_second(k):
            copy.wait_recv()
        y_red[k, 0, :, 0:4] += y_in2[k, 0]
        y_red[k, 0, :, 4:8] += y_in2[k, 1]
        for copy in z_copies(k):
            copy.start()

    def z_done(k):
        for copy in z_copies(k):
            copy.wait_recv()
        rows = pl.ds(k * CHUNK, CHUNK)
        gathered[core, zl, rows] = y_red[k, 0, zh] + z_in[k, 1]
        gathered[core, 1 - zl, rows] = z_in[k, 0] + z_in[k, 2]
        core_copy(k).start()

    def prepare_x():
        for copy in fx_copies:
            copy.wait_recv()
        entry = lax.broadcasted_iota(jnp.int32, (128, 512), 0)
        wanted = zl * 256 + (entry // 32) * 64 + core * 32 + entry % 32
        picked = (lax.broadcasted_iota(jnp.int32, (128, 512), 1) == wanted).astype(jnp.bfloat16)
        high, low = (
            lax.dot_general(picked, part, turned, preferred_element_type=jnp.float32).astype(jnp.bfloat16)
            for part in split(fx_all[...].reshape(256, 512))
        )
        fx_t[...] = jnp.concatenate([high, high, low], axis=1)

    def step(t, carry):
        pl.when(t < CHUNKS)(lambda: first_stage((t + CHUNKS - 1) % CHUNKS))
        pl.when((t >= 2) & (t < CHUNKS + 2))(lambda: second_stage(t - 2))
        pl.when(t == CHUNKS + 1)(prepare_x)
        pl.when((t >= 4) & (t < CHUNKS + 4))(lambda: y_first_done(t - 4))
        pl.when((t >= 6) & (t < CHUNKS + 6))(lambda: y_second_done(t - 6))
        pl.when(t >= 8)(lambda: z_done(t - 8))
        return carry

    lax.fori_loop(0, CHUNKS + 8, step, 0)

    for k in range(CHUNKS):
        core_copy(k).wait_recv()
    for b in range(0, 8, 2):
        pair = jnp.concatenate(
            [gathered[:, :, :, b + j, :].reshape(256, LANES) for j in range(2)], axis=1
        )
        high, low = split(pair)
        stacked = jnp.concatenate([high, low, high], axis=0)
        both = jnp.dot(fx_t[...], stacked, preferred_element_type=jnp.float32)
        for owner in range(4):
            for j in range(2):
                x_out[owner, b + j] = both[owner * 32 : owner * 32 + 32, j * LANES : (j + 1) * LANES]
    x_copies = [
        remote(x_out.at[(x + 1 + i) % 4], x_in.at[i], xr_send.at[i], xr_recv.at[i], to) for i, to in enumerate(x_peers)
    ]
    for copy in x_copies:
        copy.start()
    for copy in x_copies:
        copy.wait_recv()
    for b in range(8):
        core_out[:, b, :] = (x_out[x, b] + x_in[0, b]) + (x_in[1, b] + x_in[2, b])

    for copy in (s_low, s_high, m_low, m_high, *fx_copies, *x_copies):
        copy.wait_send()

    def drain(k, carry):
        for copy in (
            *y_faces(faces_s, halo_s, fs_send, fs_recv, k),
            *y_faces(faces_m, halo_m, fm_send, fm_recv, k),
            *y_first(k), *y_second(k), *z_copies(k), core_copy(k),
        ):
            copy.wait_send()
        return carry

    lax.fori_loop(0, CHUNKS, drain, 0)


def on_device(scalar, prefactor, factor_x, factor_y, factor_z):
    f32, bf16 = jnp.float32, jnp.bfloat16
    dma = pltpu.SemaphoreType.DMA
    vmem = pltpu.VMEM
    padded = vmem((PLANES + 2, PARTS, ROWS + 16, LANES), f32)
    faces = vmem((2, PLANES * PARTS, LANES), f32)
    anywhere = pl.BlockSpec(memory_space=pl.ANY)
    return pl.pallas_call(
        kernel,
        out_shape=(
            jax.ShapeDtypeStruct((PLANES, ROWS, PARTS * LANES), f32),
            jax.ShapeDtypeStruct((32, 8, LANES), f32),
        ),
        in_specs=[anywhere] * 5,
        out_specs=(pl.BlockSpec(memory_space=vmem), pl.BlockSpec(memory_space=vmem)),
        scratch_shapes=[
            padded, padded, vmem((PLANES, ROWS, PARTS * LANES), f32), vmem((CHUNK, ROWS, PARTS * LANES), bf16),
            vmem((512, 128), bf16), vmem((64, 64), f32), vmem((2, 2, 64, 512), f32),
            vmem((64, 192), bf16), vmem((128, 768), bf16),
            faces, faces, faces, faces,
            vmem((CHUNKS, 4, 2, CHUNK, 8, LANES), f32), vmem((CHUNKS, 2, 2, 2, 4, 8, LANES), f32),
            vmem((CHUNKS, 2, 2, 4, 8, LANES), f32), vmem((CHUNKS, 3, CHUNK, 8, LANES), f32),
            vmem((2, 2, PLANES, 8, LANES), f32), vmem((4, 8, 32, LANES), f32), vmem((3, 8, 32, LANES), f32),
            dma((CHUNKS, PARTS)), dma((CHUNKS,)), dma((3,)),
            dma((2, CHUNKS)), dma((2, CHUNKS)), dma((2, CHUNKS)), dma((2, CHUNKS)),
            dma((2,)), dma((2,)), dma((2,)), dma((2,)),
            dma((3,)), dma((3,)), dma((CHUNKS, 2)), dma((CHUNKS, 2)), dma((CHUNKS, 2)), dma((CHUNKS, 2)),
            dma((CHUNKS, 3)), dma((CHUNKS, 3)), dma((CHUNKS,)), dma((CHUNKS,)), dma((3,)), dma((3,)),
        ],
        compiler_params=pltpu.CompilerParams(collective_id=0, has_side_effects=True, vmem_limit_bytes=50 << 20),
        name="heun_tucker",
    )(scalar, prefactor, factor_x, factor_y, factor_z)


def solution(mesh):
    return jax.shard_map(
        on_device,
        mesh=mesh,
        in_specs=(P("gx", "gy", None), P("gx", "gy", None), P("gx", None), P("gy", None), P()),
        out_specs=(P("gx", "gy", None), P("gx", "gy", None)),
        check_vma=False,
    )
```

```python
import jax
import jax.numpy as jnp
from jax import lax
from jax.experimental import pallas as pl
from jax.experimental.pallas import tpu as pltpu
from jax.sharding import PartitionSpec as P

MESH = pl.DeviceIdType.MESH
spread_rate = 0.12
activation = 2.0
PLANES, ROWS, LANES, PARTS = 64, 64, 128, 4
CHUNK = 8
CHUNKS = PLANES // CHUNK
TOP = 8
PADDED = ROWS + 16
STRIP = CHUNK * PARTS
BAND = 16
FIX = 4
SECOND = 8
FIRST_SUM, SECOND_SUM, Z_SUM = SECOND + 2, SECOND + 4, SECOND + 6


def split(value):
    high = value.astype(jnp.bfloat16)
    low = (value - high.astype(jnp.float32)).astype(jnp.bfloat16)
    return high, low


def kernel(
    scalar, prefactor, factor_x, factor_y, factor_z, advanced, core_out,
    field, middle, pref, beside_x, lowered, fz, fy, fx_all, fy_t, fx_t,
    faces_s, halo_s, faces_m, halo_m,
    y_red, y_in1, y_in2, z_in, gathered, x_out, x_in,
    load_sem, pref_sem, small_sem,
    fs_send, fs_recv, fm_send, fm_recv, xs_send, xs_recv, xm_send, xm_recv,
    fx_send, fx_recv, y1_send, y1_recv, y2_send, y2_recv, z_send, z_recv, c_send, c_recv, xr_send, xr_recv,
):
    gx, gy = lax.axis_index("gx"), lax.axis_index("gy")
    core, x, zl = gx % 2, (gx // 2) % 4, gx // 8
    y, zh = gy % 4, gy // 4

    def device(core, x, zl, y, zh):
        return (zl * 8 + x * 2 + core, zh * 4 + y)

    up_x, down_x = ((gx + 1) % 16, gy), ((gx + 15) % 16, gy)
    up_y, down_y = (gx, (gy + 1) % 8), (gx, (gy + 7) % 8)
    y_by1 = y + 1 - 2 * (y % 2)
    y_by3 = 3 - y
    pair_a, pair_b = device(core, x, zl, y_by1, zh), device(core, x, zl, y_by3, zh)
    z_peers = [device(core, x, 1 - zl, y, zh), device(core, x, zl, y, 1 - zh), device(core, x, 1 - zl, y, 1 - zh)]
    partner = device(1 - core, x, zl, y, zh)
    fx_peers = [partner, z_peers[0], device(1 - core, x, 1 - zl, y, zh)]
    x_peers = [device(core, (x + j) % 4, zl, y, zh) for j in (1, 2, 3)]

    def load(k, part):
        return pltpu.make_async_copy(
            scalar.at[pl.ds(k * CHUNK, CHUNK), :, pl.ds(part * LANES, LANES)],
            field.at[pl.ds(k * CHUNK + 1, CHUNK), part, pl.ds(TOP, ROWS), :],
            load_sem.at[k, part],
        )

    def load_pref(k):
        rows = pl.ds(k * CHUNK, CHUNK)
        return pltpu.make_async_copy(prefactor.at[rows], pref.at[rows], pref_sem.at[k])

    for part in range(PARTS):
        load(7, part).start()
        load(6, part).start()
    load_pref(7).start()
    for k in (0, 1):
        for part in range(PARTS):
            load(k, part).start()
    load_pref(0).start()
    fx_load = pltpu.make_async_copy(factor_x, fx_all.at[core, zl], small_sem.at[0])
    fz_load = pltpu.make_async_copy(factor_z, fz, small_sem.at[1])
    fy_load = pltpu.make_async_copy(factor_y, fy, small_sem.at[2])
    for k in range(2, CHUNKS - 2):
        for part in range(PARTS):
            load(k, part).start()
        load_pref(k - 1).start()
        if k == 2:
            fx_load.start()
            fz_load.start()
            fy_load.start()
    load_pref(5).start()
    load_pref(6).start()

    barrier = pltpu.get_barrier_semaphore()
    peers = [up_x, down_x, up_y, down_y, pair_a, pair_b, *z_peers, partner, fx_peers[2], *x_peers]
    for peer in peers:
        pl.semaphore_signal(barrier, inc=1, device_id=peer, device_id_type=MESH)

    def clear_plane(buffer, index):
        for part in range(PARTS):
            buffer[index, part, TOP : TOP + ROWS, :] = jnp.zeros((ROWS, LANES), jnp.float32)

    clear_plane(field, 0)
    clear_plane(field, PLANES + 1)

    def rows_of(buffer, k, row):
        start = (k * CHUNK + 1) * PARTS * PADDED + row
        return buffer.reshape((PLANES + 2) * PARTS * PADDED, LANES).at[pl.ds(start, STRIP, stride=PADDED), :]

    for k in range(CHUNKS):
        for row in (TOP - 1, TOP + ROWS):
            rows_of(field, k, row)[...] = jnp.zeros((STRIP, LANES), jnp.float32)
    pl.semaphore_wait(barrier, len(peers))

    def remote(src, dst, send, recv, to):
        return pltpu.make_async_remote_copy(
            src_ref=src, dst_ref=dst, send_sem=send, recv_sem=recv, device_id=to, device_id_type=MESH
        )

    def plane_of(buffer, index):
        return buffer.at[index, :, pl.ds(TOP, ROWS), :]

    def y_faces(faces, halo, send, recv, k):
        rows = pl.ds(k * STRIP, STRIP)
        low = remote(faces.at[0, rows], halo.at[1, rows], send.at[0, k], recv.at[0, k], down_y)
        high = remote(faces.at[1, rows], halo.at[0, rows], send.at[1, k], recv.at[1, k], up_y)
        return low, high

    s_low = remote(plane_of(field, 1), beside_x.at[1], xs_send.at[0], xs_recv.at[0], down_x)
    s_high = remote(plane_of(field, PLANES), beside_x.at[0], xs_send.at[1], xs_recv.at[1], up_x)
    m_low = remote(plane_of(middle, 1), plane_of(middle, PLANES + 1), xm_send.at[0], xm_recv.at[0], down_x)
    m_high = remote(plane_of(middle, PLANES), plane_of(middle, 0), xm_send.at[1], xm_recv.at[1], up_x)

    def send_faces(k):
        for part in range(PARTS):
            load(k, part).wait()
        faces_s[0, pl.ds(k * STRIP, STRIP), :] = rows_of(field, k, TOP)[...]
        faces_s[1, pl.ds(k * STRIP, STRIP), :] = rows_of(field, k, TOP + ROWS - 1)[...]
        for copy in y_faces(faces_s, halo_s, fs_send, fs_recv, k):
            copy.start()

    send_faces(7)
    s_high.start()
    send_faces(6)

    fx_copies = [
        remote(fx_all.at[core, zl], fx_all.at[core, zl], fx_send.at[i], fx_recv.at[i], to)
        for i, to in enumerate(fx_peers)
    ]
    fx_load.wait()
    fz_load.wait()
    fy_load.wait()
    eye = (
        lax.broadcasted_iota(jnp.int32, (64, 64), 0) == lax.broadcasted_iota(jnp.int32, (64, 64), 1)
    ).astype(jnp.bfloat16)
    turned = (((1,), (1,)), ((), ()))
    fy_high, fy_low = (
        lax.dot_general(eye, part, turned, preferred_element_type=jnp.float32).astype(jnp.bfloat16)
        for part in split(fy[...])
    )
    fy_t[...] = jnp.concatenate([fy_high, fy_high, fy_low], axis=1)

    lane = lax.broadcasted_iota(jnp.int32, (BAND, LANES), 1)
    at_left, at_right = lane == 0, lane == LANES - 1

    def stepped(buffer, plane, row):
        at = plane + 1
        own = slice(TOP + row, TOP + row + BAND)
        centers = [buffer[at, part, own, :] for part in range(PARTS)]
        lefts = [pltpu.roll(c, 1, 1) for c in centers]
        rights = [pltpu.roll(c, LANES - 1, 1) for c in centers]
        results = []
        for part, c in enumerate(centers):
            left = jnp.where(at_left, lefts[part - 1] if part > 0 else 0.0, lefts[part])
            right = jnp.where(at_right, rights[part + 1] if part + 1 < PARTS else 0.0, rights[part])
            beside = buffer[at + 1, part, own, :] + buffer[at - 1, part, own, :]
            beside = beside + (
                buffer[at, part, TOP + row + 1 : TOP + row + 1 + BAND, :]
                + buffer[at, part, TOP + row - 1 : TOP + row - 1 + BAND, :]
            )
            beside = beside + (left + right)
            factor = pref[plane, row : row + BAND, part * LANES : (part + 1) * LANES]
            source = factor * jnp.exp(-activation / (1.0 + c * c))
            results.append((1.0 - 6.0 * spread_rate) * c + spread_rate * beside + source)
        return results

    def first_stage(k):
        load_pref(k).wait()

        def plane_step(i, carry):
            plane = k * CHUNK + i
            for row in range(0, ROWS, BAND):
                for part, value in enumerate(stepped(field, plane, row)):
                    middle[plane + 1, part, TOP + row : TOP + row + BAND, :] = value
            return carry

        lax.fori_loop(0, CHUNK, plane_step, 0)

    def add_x(plane, side, inside):
        for part in range(PARTS):
            own = (plane + 1, part, slice(TOP, TOP + ROWS), slice(None))
            middle[own] = middle[own] + spread_rate * jnp.where(inside, beside_x[side, part], 0.0)

    def add_halo(k):
        @pl.when(k == CHUNKS - 1)
        def _():
            s_low.wait_recv()
            add_x(PLANES - 1, 1, gx < 15)

        @pl.when(k == 0)
        def _():
            s_high.wait_recv()
            add_x(0, 0, gx > 0)

        for copy in y_faces(faces_s, halo_s, fs_send, fs_recv, k):
            copy.wait_recv()
        rows = pl.ds(k * STRIP, STRIP)
        for side, inside, row in ((0, gy > 0, TOP), (1, gy < 7, TOP + ROWS - 1)):
            edge = rows_of(middle, k, row)
            value = edge[...] + spread_rate * jnp.where(inside, halo_s[side, rows, :], 0.0)
            faces_m[side, rows, :] = value
            edge[...] = value
        for copy in y_faces(faces_m, halo_m, fm_send, fm_recv, k):
            copy.start()

        @pl.when(k == CHUNKS - 1)
        def _():
            m_high.start()

        @pl.when(k == 0)
        def _():
            m_low.start()

    def y_first(k):
        a = remote(y_red.at[k, pl.ds(1, 2), :, pl.ds(0, 4)], y_in1.at[k, 0], y1_send.at[k, 0], y1_recv.at[k, 0], pair_a)
        b = remote(y_red.at[k, pl.ds(2, 2), :, pl.ds(4, 4)], y_in1.at[k, 1], y1_send.at[k, 1], y1_recv.at[k, 1], pair_b)
        return a, b

    def y_second(k):
        a = remote(y_red.at[k, 3, :, pl.ds(0, 4)], y_in2.at[k, 0], y2_send.at[k, 0], y2_recv.at[k, 0], pair_b)
        b = remote(y_red.at[k, 1, :, pl.ds(4, 4)], y_in2.at[k, 1], y2_send.at[k, 1], y2_recv.at[k, 1], pair_a)
        return a, b

    def z_copies(k):
        return [
            remote(y_red.at[k, 0, block], z_in.at[k, i], z_send.at[k, i], z_recv.at[k, i], z_peers[i])
            for i, block in enumerate((zh, 1 - zh, 1 - zh))
        ]

    def core_copy(k):
        block = gathered.at[core, :, pl.ds(k * CHUNK, CHUNK)]
        return remote(block, block, c_send.at[k], c_recv.at[k], partner)

    def second_stage(k):
        low, high = y_faces(faces_m, halo_m, fm_send, fm_recv, k)
        low.wait_recv()
        high.wait_recv()

        @pl.when(k == CHUNKS - 1)
        def _():
            m_low.wait_recv()

            @pl.when(gx == 15)
            def _():
                clear_plane(middle, PLANES + 1)

        @pl.when(k == 0)
        def _():
            m_high.wait_recv()

            @pl.when(gx == 0)
            def _():
                clear_plane(middle, 0)

        rows = pl.ds(k * STRIP, STRIP)
        rows_of(middle, k, TOP - 1)[...] = jnp.where(gy > 0, halo_m[0, rows, :], 0.0)
        rows_of(middle, k, TOP + ROWS)[...] = jnp.where(gy < 7, halo_m[1, rows, :], 0.0)

        def plane_step(i, carry):
            plane = k * CHUNK + i
            for row in range(0, ROWS, BAND):
                for part, value in enumerate(stepped(middle, plane, row)):
                    value = 0.5 * (field[plane + 1, part, TOP + row : TOP + row + BAND, :] + value)
                    lanes = slice(part * LANES, (part + 1) * LANES)
                    advanced[plane, row : row + BAND, lanes] = value
                    lowered[i, row : row + BAND, lanes] = value.astype(jnp.bfloat16)
            return carry

        lax.fori_loop(0, CHUNK, plane_step, 0)
        z_red = jnp.dot(
            lowered[...].reshape(CHUNK * ROWS, PARTS * LANES), fz[...], preferred_element_type=jnp.float32
        )
        blocks = [y, y_by1, (y + 2) % 4, y_by3]
        for i in range(0, CHUNK, 2):
            pair = jnp.concatenate([z_red[i * ROWS : (i + 1) * ROWS], z_red[(i + 1) * ROWS : (i + 2) * ROWS]], axis=1)
            high, low = split(pair)
            stacked = jnp.concatenate([high, low, high], axis=0)
            both = jnp.dot(fy_t[...], stacked, preferred_element_type=jnp.float32)
            for owner in range(8):
                for j in range(2):
                    y_red[k, blocks[owner % 4], owner // 4, i + j] = both[
                        owner * 8 : owner * 8 + 8, j * LANES : (j + 1) * LANES
                    ]
        for copy in y_first(k):
            copy.start()

    def y_first_done(k):
        for copy in y_first(k):
            copy.wait_recv()
        y_red[k, 0, :, 0:4] += y_in1[k, 0, 0]
        y_red[k, 3, :, 0:4] += y_in1[k, 0, 1]
        y_red[k, 1, :, 4:8] += y_in1[k, 1, 0]
        y_red[k, 0, :, 4:8] += y_in1[k, 1, 1]
        for copy in y_second(k):
            copy.start()

    def y_second_done(k):
        for copy in y_second(k):
            copy.wait_recv()
        y_red[k, 0, :, 0:4] += y_in2[k, 0]
        y_red[k, 0, :, 4:8] += y_in2[k, 1]
        for copy in z_copies(k):
            copy.start()

    def z_done(k):
        for copy in z_copies(k):
            copy.wait_recv()
        rows = pl.ds(k * CHUNK, CHUNK)
        gathered[core, zl, rows] = y_red[k, 0, zh] + z_in[k, 1]
        gathered[core, 1 - zl, rows] = z_in[k, 0] + z_in[k, 2]
        core_copy(k).start()

    def prepare_x():
        for copy in fx_copies:
            copy.wait_recv()
        entry = lax.broadcasted_iota(jnp.int32, (128, 512), 0)
        wanted = zl * 256 + (entry // 32) * 64 + core * 32 + entry % 32
        picked = (lax.broadcasted_iota(jnp.int32, (128, 512), 1) == wanted).astype(jnp.bfloat16)
        high, low = (
            lax.dot_general(picked, part, turned, preferred_element_type=jnp.float32).astype(jnp.bfloat16)
            for part in split(fx_all[...].reshape(256, 512))
        )
        fx_t[...] = jnp.concatenate([high, high, low], axis=1)

    def step(t, carry):
        pl.when(t < CHUNKS - 2)(lambda: send_faces(t))

        @pl.when(t == 0)
        def _():
            s_low.start()

        @pl.when(t == 3)
        def _():
            for copy in fx_copies:
                copy.start()

        pl.when(t < CHUNKS)(lambda: first_stage((t + CHUNKS - 1) % CHUNKS))
        pl.when((t >= FIX) & (t < CHUNKS + FIX))(lambda: add_halo((t - FIX + CHUNKS - 1) % CHUNKS))
        pl.when((t >= SECOND) & (t < CHUNKS + SECOND))(lambda: second_stage(t - SECOND))
        pl.when((t >= FIRST_SUM) & (t < CHUNKS + FIRST_SUM))(lambda: y_first_done(t - FIRST_SUM))
        pl.when((t >= SECOND_SUM) & (t < CHUNKS + SECOND_SUM))(lambda: y_second_done(t - SECOND_SUM))
        pl.when(t == CHUNKS + SECOND)(prepare_x)
        pl.when(t >= Z_SUM)(lambda: z_done(t - Z_SUM))
        return carry

    lax.fori_loop(0, CHUNKS + Z_SUM, step, 0)

    for k in range(CHUNKS):
        core_copy(k).wait_recv()
    for b in range(0, 8, 2):
        pair = jnp.concatenate(
            [gathered[:, :, :, b + j, :].reshape(256, LANES) for j in range(2)], axis=1
        )
        high, low = split(pair)
        stacked = jnp.concatenate([high, low, high], axis=0)
        both = jnp.dot(fx_t[...], stacked, preferred_element_type=jnp.float32)
        for owner in range(4):
            for j in range(2):
                x_out[owner, b + j] = both[owner * 32 : owner * 32 + 32, j * LANES : (j + 1) * LANES]
    x_copies = [
        remote(x_out.at[(x + 1 + i) % 4], x_in.at[i], xr_send.at[i], xr_recv.at[i], to) for i, to in enumerate(x_peers)
    ]
    for copy in x_copies:
        copy.start()
    for copy in x_copies:
        copy.wait_recv()
    for b in range(8):
        core_out[:, b, :] = (x_out[x, b] + x_in[0, b]) + (x_in[1, b] + x_in[2, b])

    for copy in (s_low, s_high, m_low, m_high, *fx_copies, *x_copies):
        copy.wait_send()

    def drain(k, carry):
        for copy in (
            *y_faces(faces_s, halo_s, fs_send, fs_recv, k),
            *y_faces(faces_m, halo_m, fm_send, fm_recv, k),
            *y_first(k), *y_second(k), *z_copies(k), core_copy(k),
        ):
            copy.wait_send()
        return carry

    lax.fori_loop(0, CHUNKS, drain, 0)


def on_device(scalar, prefactor, factor_x, factor_y, factor_z):
    f32, bf16 = jnp.float32, jnp.bfloat16
    dma = pltpu.SemaphoreType.DMA
    vmem = pltpu.VMEM
    padded = vmem((PLANES + 2, PARTS, PADDED, LANES), f32)
    faces = vmem((2, PLANES * PARTS, LANES), f32)
    anywhere = pl.BlockSpec(memory_space=pl.ANY)
    return pl.pallas_call(
        kernel,
        out_shape=(
            jax.ShapeDtypeStruct((PLANES, ROWS, PARTS * LANES), f32),
            jax.ShapeDtypeStruct((32, 8, LANES), f32),
        ),
        in_specs=[anywhere] * 5,
        out_specs=(pl.BlockSpec(memory_space=vmem), pl.BlockSpec(memory_space=vmem)),
        scratch_shapes=[
            padded, padded, vmem((PLANES, ROWS, PARTS * LANES), f32), vmem((2, PARTS, ROWS, LANES), f32), vmem((CHUNK, ROWS, PARTS * LANES), bf16),
            vmem((512, 128), bf16), vmem((64, 64), f32), vmem((2, 2, 64, 512), f32),
            vmem((64, 192), bf16), vmem((128, 768), bf16),
            faces, faces, faces, faces,
            vmem((CHUNKS, 4, 2, CHUNK, 8, LANES), f32), vmem((CHUNKS, 2, 2, 2, 4, 8, LANES), f32),
            vmem((CHUNKS, 2, 2, 4, 8, LANES), f32), vmem((CHUNKS, 3, CHUNK, 8, LANES), f32),
            vmem((2, 2, PLANES, 8, LANES), f32), vmem((4, 8, 32, LANES), f32), vmem((3, 8, 32, LANES), f32),
            dma((CHUNKS, PARTS)), dma((CHUNKS,)), dma((3,)),
            dma((2, CHUNKS)), dma((2, CHUNKS)), dma((2, CHUNKS)), dma((2, CHUNKS)),
            dma((2,)), dma((2,)), dma((2,)), dma((2,)),
            dma((3,)), dma((3,)), dma((CHUNKS, 2)), dma((CHUNKS, 2)), dma((CHUNKS, 2)), dma((CHUNKS, 2)),
            dma((CHUNKS, 3)), dma((CHUNKS, 3)), dma((CHUNKS,)), dma((CHUNKS,)), dma((3,)), dma((3,)),
        ],
        compiler_params=pltpu.CompilerParams(collective_id=0, has_side_effects=True, vmem_limit_bytes=40 << 20),
        name="heun_tucker",
    )(scalar, prefactor, *(pltpu.with_memory_space_constraint(a, pltpu.HBM) for a in (factor_x, factor_y, factor_z)))


def solution(mesh):
    return jax.shard_map(
        on_device,
        mesh=mesh,
        in_specs=(P("gx", "gy", None), P("gx", "gy", None), P("gx", None), P("gy", None), P()),
        out_specs=(P("gx", "gy", None), P("gx", "gy", None)),
        check_vma=False,
    )
```

```python
import jax
import jax.numpy as jnp
from jax import lax
from jax.experimental import pallas as pl
from jax.experimental.pallas import tpu as pltpu
from jax.sharding import PartitionSpec as P

MESH = pl.DeviceIdType.MESH
spread_rate = 0.12
activation = 2.0
PLANES, ROWS, LANES, PARTS = 64, 64, 128, 4
CHUNK = 8
CHUNKS = PLANES // CHUNK
TOP = 8
PADDED = ROWS + 16
STRIP = CHUNK * PARTS
GROUP = 8
BAND = 16
FIX = 4
SECOND = 8
FIRST_SUM, SECOND_SUM, Z_SUM = SECOND + 2, SECOND + 4, SECOND + 6


def split(value):
    high = value.astype(jnp.bfloat16)
    low = (value - high.astype(jnp.float32)).astype(jnp.bfloat16)
    return high, low


def kernel(
    scalar, prefactor, factor_x, factor_y, factor_z, advanced, core_out,
    field, middle, pref, beside_x, band, lowered, fz, fy, fx_all, fy_t, fx_t,
    faces_s, halo_s, faces_m, halo_m,
    y_red, y_in1, y_in2, z_in, gathered, x_out, x_in,
    load_sem, pref_sem, small_sem,
    fs_send, fs_recv, fm_send, fm_recv, xs_send, xs_recv, xm_send, xm_recv,
    fx_send, fx_recv, y1_send, y1_recv, y2_send, y2_recv, z_send, z_recv, c_send, c_recv, xr_send, xr_recv,
):
    gx, gy = lax.axis_index("gx"), lax.axis_index("gy")
    core, x, zl = gx % 2, (gx // 2) % 4, gx // 8
    y, zh = gy % 4, gy // 4

    def device(core, x, zl, y, zh):
        return (zl * 8 + x * 2 + core, zh * 4 + y)

    up_x, down_x = ((gx + 1) % 16, gy), ((gx + 15) % 16, gy)
    up_y, down_y = (gx, (gy + 1) % 8), (gx, (gy + 7) % 8)
    y_by1 = y + 1 - 2 * (y % 2)
    y_by3 = 3 - y
    pair_a, pair_b = device(core, x, zl, y_by1, zh), device(core, x, zl, y_by3, zh)
    z_peers = [device(core, x, 1 - zl, y, zh), device(core, x, zl, y, 1 - zh), device(core, x, 1 - zl, y, 1 - zh)]
    partner = device(1 - core, x, zl, y, zh)
    fx_peers = [partner, z_peers[0], device(1 - core, x, 1 - zl, y, zh)]
    x_peers = [device(core, (x + j) % 4, zl, y, zh) for j in (1, 2, 3)]

    def load(k, part):
        return pltpu.make_async_copy(
            scalar.at[pl.ds(k * CHUNK, CHUNK), :, pl.ds(part * LANES, LANES)],
            field.at[pl.ds(k * CHUNK + 1, CHUNK), part, pl.ds(TOP, ROWS), :],
            load_sem.at[k, part],
        )

    def load_pref(k):
        rows = pl.ds(k * CHUNK, CHUNK)
        return pltpu.make_async_copy(prefactor.at[rows], pref.at[rows], pref_sem.at[k])

    for part in range(PARTS):
        load(7, part).start()
        load(6, part).start()
    load_pref(7).start()
    for k in (0, 1):
        for part in range(PARTS):
            load(k, part).start()
    load_pref(0).start()
    fx_load = pltpu.make_async_copy(factor_x, fx_all.at[core, zl], small_sem.at[0])
    fz_load = pltpu.make_async_copy(factor_z, fz, small_sem.at[1])
    fy_load = pltpu.make_async_copy(factor_y, fy, small_sem.at[2])
    for k in range(2, CHUNKS - 2):
        for part in range(PARTS):
            load(k, part).start()
        load_pref(k - 1).start()
        if k == 2:
            fx_load.start()
            fz_load.start()
            fy_load.start()
    load_pref(5).start()
    load_pref(6).start()

    barrier = pltpu.get_barrier_semaphore()
    peers = [up_x, down_x, up_y, down_y, pair_a, pair_b, *z_peers, partner, fx_peers[2], *x_peers]
    for peer in peers:
        pl.semaphore_signal(barrier, inc=1, device_id=peer, device_id_type=MESH)

    def clear_plane(buffer, index):
        for part in range(PARTS):
            buffer[index, part, TOP : TOP + ROWS, :] = jnp.zeros((ROWS, LANES), jnp.float32)

    clear_plane(field, 0)
    clear_plane(field, PLANES + 1)

    def rows_of(buffer, k, row):
        start = (k * CHUNK + 1) * PARTS * PADDED + row
        return buffer.reshape((PLANES + 2) * PARTS * PADDED, LANES).at[pl.ds(start, STRIP, stride=PADDED), :]

    for k in range(CHUNKS):
        for row in (TOP - 1, TOP + ROWS):
            rows_of(field, k, row)[...] = jnp.zeros((STRIP, LANES), jnp.float32)
    along = lax.broadcasted_iota(jnp.int32, (512, 512), 0)
    across = lax.broadcasted_iota(jnp.int32, (512, 512), 1)
    band[...] = ((along == across + 1) | (across == along + 1)).astype(jnp.bfloat16)
    pl.semaphore_wait(barrier, len(peers))

    def remote(src, dst, send, recv, to):
        return pltpu.make_async_remote_copy(
            src_ref=src, dst_ref=dst, send_sem=send, recv_sem=recv, device_id=to, device_id_type=MESH
        )

    def plane_of(buffer, index):
        return buffer.at[index, :, pl.ds(TOP, ROWS), :]

    def y_faces(faces, halo, send, recv, k):
        rows = pl.ds(k * STRIP, STRIP)
        low = remote(faces.at[0, rows], halo.at[1, rows], send.at[0, k], recv.at[0, k], down_y)
        high = remote(faces.at[1, rows], halo.at[0, rows], send.at[1, k], recv.at[1, k], up_y)
        return low, high

    s_low = remote(plane_of(field, 1), beside_x.at[1], xs_send.at[0], xs_recv.at[0], down_x)
    s_high = remote(plane_of(field, PLANES), beside_x.at[0], xs_send.at[1], xs_recv.at[1], up_x)
    m_low = remote(plane_of(middle, 1), plane_of(middle, PLANES + 1), xm_send.at[0], xm_recv.at[0], down_x)
    m_high = remote(plane_of(middle, PLANES), plane_of(middle, 0), xm_send.at[1], xm_recv.at[1], up_x)

    def send_faces(k):
        for part in range(PARTS):
            load(k, part).wait()
        faces_s[0, pl.ds(k * STRIP, STRIP), :] = rows_of(field, k, TOP)[...]
        faces_s[1, pl.ds(k * STRIP, STRIP), :] = rows_of(field, k, TOP + ROWS - 1)[...]
        for copy in y_faces(faces_s, halo_s, fs_send, fs_recv, k):
            copy.start()

    send_faces(7)
    s_high.start()
    send_faces(6)

    fx_copies = [
        remote(fx_all.at[core, zl], fx_all.at[core, zl], fx_send.at[i], fx_recv.at[i], to)
        for i, to in enumerate(fx_peers)
    ]
    fx_load.wait()
    fz_load.wait()
    fy_load.wait()
    eye = (
        lax.broadcasted_iota(jnp.int32, (64, 64), 0) == lax.broadcasted_iota(jnp.int32, (64, 64), 1)
    ).astype(jnp.bfloat16)
    turned = (((1,), (1,)), ((), ()))
    fy_high, fy_low = (
        lax.dot_general(eye, part, turned, preferred_element_type=jnp.float32).astype(jnp.bfloat16)
        for part in split(fy[...])
    )
    fy_t[...] = jnp.concatenate([fy_high, fy_high, fy_low], axis=1)

    def beside_z(buffer, plane):
        planes = [
            jnp.concatenate([buffer[plane + i + 1, part, TOP : TOP + ROWS, :] for part in range(PARTS)], axis=1)
            for i in range(GROUP)
        ]
        return jnp.dot(
            jnp.concatenate(planes, axis=0).astype(jnp.bfloat16), band[...], preferred_element_type=jnp.float32
        )

    def stepped(buffer, plane, row, sums):
        at = plane + 1
        own = slice(TOP + row, TOP + row + BAND)
        centers = [buffer[at, part, own, :] for part in range(PARTS)]
        results = []
        for part, c in enumerate(centers):
            beside = buffer[at + 1, part, own, :] + buffer[at - 1, part, own, :]
            beside = beside + (
                buffer[at, part, TOP + row + 1 : TOP + row + 1 + BAND, :]
                + buffer[at, part, TOP + row - 1 : TOP + row - 1 + BAND, :]
            )
            beside = beside + sums[row : row + BAND, part * LANES : (part + 1) * LANES]
            factor = pref[plane, row : row + BAND, part * LANES : (part + 1) * LANES]
            source = factor * jnp.exp(-activation / (1.0 + c * c))
            results.append((1.0 - 6.0 * spread_rate) * c + spread_rate * beside + source)
        return results

    def first_stage(k):
        load_pref(k).wait()

        def group_step(g, carry):
            start = k * CHUNK + g * GROUP
            sums = beside_z(field, start)
            for i in range(GROUP):
                plane = start + i
                for row in range(0, ROWS, BAND):
                    for part, value in enumerate(stepped(field, plane, row, sums[i * ROWS : (i + 1) * ROWS])):
                        middle[plane + 1, part, TOP + row : TOP + row + BAND, :] = value
            return carry

        lax.fori_loop(0, CHUNK // GROUP, group_step, 0)

    def add_x(plane, side, inside):
        for part in range(PARTS):
            own = (plane + 1, part, slice(TOP, TOP + ROWS), slice(None))
            middle[own] = middle[own] + spread_rate * jnp.where(inside, beside_x[side, part], 0.0)

    def add_halo(k):
        @pl.when(k == CHUNKS - 1)
        def _():
            s_low.wait_recv()
            add_x(PLANES - 1, 1, gx < 15)

        @pl.when(k == 0)
        def _():
            s_high.wait_recv()
            add_x(0, 0, gx > 0)

        for copy in y_faces(faces_s, halo_s, fs_send, fs_recv, k):
            copy.wait_recv()
        rows = pl.ds(k * STRIP, STRIP)
        for side, inside, row in ((0, gy > 0, TOP), (1, gy < 7, TOP + ROWS - 1)):
            edge = rows_of(middle, k, row)
            value = edge[...] + spread_rate * jnp.where(inside, halo_s[side, rows, :], 0.0)
            faces_m[side, rows, :] = value
            edge[...] = value
        for copy in y_faces(faces_m, halo_m, fm_send, fm_recv, k):
            copy.start()

        @pl.when(k == CHUNKS - 1)
        def _():
            m_high.start()

        @pl.when(k == 0)
        def _():
            m_low.start()

    def y_first(k):
        a = remote(y_red.at[k, pl.ds(1, 2), :, pl.ds(0, 4)], y_in1.at[k, 0], y1_send.at[k, 0], y1_recv.at[k, 0], pair_a)
        b = remote(y_red.at[k, pl.ds(2, 2), :, pl.ds(4, 4)], y_in1.at[k, 1], y1_send.at[k, 1], y1_recv.at[k, 1], pair_b)
        return a, b

    def y_second(k):
        a = remote(y_red.at[k, 3, :, pl.ds(0, 4)], y_in2.at[k, 0], y2_send.at[k, 0], y2_recv.at[k, 0], pair_b)
        b = remote(y_red.at[k, 1, :, pl.ds(4, 4)], y_in2.at[k, 1], y2_send.at[k, 1], y2_recv.at[k, 1], pair_a)
        return a, b

    def z_copies(k):
        return [
            remote(y_red.at[k, 0, block], z_in.at[k, i], z_send.at[k, i], z_recv.at[k, i], z_peers[i])
            for i, block in enumerate((zh, 1 - zh, 1 - zh))
        ]

    def core_copy(k):
        block = gathered.at[core, :, pl.ds(k * CHUNK, CHUNK)]
        return remote(block, block, c_send.at[k], c_recv.at[k], partner)

    def second_stage(k):
        low, high = y_faces(faces_m, halo_m, fm_send, fm_recv, k)
        low.wait_recv()
        high.wait_recv()

        @pl.when(k == CHUNKS - 1)
        def _():
            m_low.wait_recv()

            @pl.when(gx == 15)
            def _():
                clear_plane(middle, PLANES + 1)

        @pl.when(k == 0)
        def _():
            m_high.wait_recv()

            @pl.when(gx == 0)
            def _():
                clear_plane(middle, 0)

        rows = pl.ds(k * STRIP, STRIP)
        rows_of(middle, k, TOP - 1)[...] = jnp.where(gy > 0, halo_m[0, rows, :], 0.0)
        rows_of(middle, k, TOP + ROWS)[...] = jnp.where(gy < 7, halo_m[1, rows, :], 0.0)

        def group_step(g, carry):
            start = k * CHUNK + g * GROUP
            sums = beside_z(middle, start)
            for i in range(GROUP):
                plane = start + i
                for row in range(0, ROWS, BAND):
                    for part, value in enumerate(stepped(middle, plane, row, sums[i * ROWS : (i + 1) * ROWS])):
                        value = 0.5 * (field[plane + 1, part, TOP + row : TOP + row + BAND, :] + value)
                        lanes = slice(part * LANES, (part + 1) * LANES)
                        advanced[plane, row : row + BAND, lanes] = value
                        lowered[g * GROUP + i, row : row + BAND, lanes] = value.astype(jnp.bfloat16)
            return carry

        lax.fori_loop(0, CHUNK // GROUP, group_step, 0)
        z_red = jnp.dot(
            lowered[...].reshape(CHUNK * ROWS, PARTS * LANES), fz[...], preferred_element_type=jnp.float32
        )
        blocks = [y, y_by1, (y + 2) % 4, y_by3]
        for i in range(0, CHUNK, 2):
            pair = jnp.concatenate([z_red[i * ROWS : (i + 1) * ROWS], z_red[(i + 1) * ROWS : (i + 2) * ROWS]], axis=1)
            high, low = split(pair)
            stacked = jnp.concatenate([high, low, high], axis=0)
            both = jnp.dot(fy_t[...], stacked, preferred_element_type=jnp.float32)
            for owner in range(8):
                for j in range(2):
                    y_red[k, blocks[owner % 4], owner // 4, i + j] = both[
                        owner * 8 : owner * 8 + 8, j * LANES : (j + 1) * LANES
                    ]
        for copy in y_first(k):
            copy.start()

    def y_first_done(k):
        for copy in y_first(k):
            copy.wait_recv()
        y_red[k, 0, :, 0:4] += y_in1[k, 0, 0]
        y_red[k, 3, :, 0:4] += y_in1[k, 0, 1]
        y_red[k, 1, :, 4:8] += y_in1[k, 1, 0]
        y_red[k, 0, :, 4:8] += y_in1[k, 1, 1]
        for copy in y_second(k):
            copy.start()

    def y_second_done(k):
        for copy in y_second(k):
            copy.wait_recv()
        y_red[k, 0, :, 0:4] += y_in2[k, 0]
        y_red[k, 0, :, 4:8] += y_in2[k, 1]
        for copy in z_copies(k):
            copy.start()

    def z_done(k):
        for copy in z_copies(k):
            copy.wait_recv()
        rows = pl.ds(k * CHUNK, CHUNK)
        gathered[core, zl, rows] = y_red[k, 0, zh] + z_in[k, 1]
        gathered[core, 1 - zl, rows] = z_in[k, 0] + z_in[k, 2]
        core_copy(k).start()

    def prepare_x():
        for copy in fx_copies:
            copy.wait_recv()
        entry = lax.broadcasted_iota(jnp.int32, (128, 512), 0)
        wanted = zl * 256 + (entry // 32) * 64 + core * 32 + entry % 32
        picked = (lax.broadcasted_iota(jnp.int32, (128, 512), 1) == wanted).astype(jnp.bfloat16)
        high, low = (
            lax.dot_general(picked, part, turned, preferred_element_type=jnp.float32).astype(jnp.bfloat16)
            for part in split(fx_all[...].reshape(256, 512))
        )
        fx_t[...] = jnp.concatenate([high, high, low], axis=1)

    def step(t, carry):
        pl.when(t < CHUNKS - 2)(lambda: send_faces(t))

        @pl.when(t == 0)
        def _():
            s_low.start()

        @pl.when(t == 3)
        def _():
            for copy in fx_copies:
                copy.start()

        pl.when(t < CHUNKS)(lambda: first_stage((t + CHUNKS - 1) % CHUNKS))
        pl.when((t >= FIX) & (t < CHUNKS + FIX))(lambda: add_halo((t - FIX + CHUNKS - 1) % CHUNKS))
        pl.when((t >= SECOND) & (t < CHUNKS + SECOND))(lambda: second_stage(t - SECOND))
        pl.when((t >= FIRST_SUM) & (t < CHUNKS + FIRST_SUM))(lambda: y_first_done(t - FIRST_SUM))
        pl.when((t >= SECOND_SUM) & (t < CHUNKS + SECOND_SUM))(lambda: y_second_done(t - SECOND_SUM))
        pl.when(t == CHUNKS + SECOND)(prepare_x)
        pl.when(t >= Z_SUM)(lambda: z_done(t - Z_SUM))
        return carry

    lax.fori_loop(0, CHUNKS + Z_SUM, step, 0)

    def x_pair(b):
        rows = pl.ds(b, 2)
        return [
            remote(
                x_out.at[(x + 1 + i) % 4, rows], x_in.at[i, rows], xr_send.at[i, b // 2], xr_recv.at[i, b // 2], to
            )
            for i, to in enumerate(x_peers)
        ]

    for k in range(CHUNKS):
        core_copy(k).wait_recv()
    for b in range(0, 8, 2):
        pair = jnp.concatenate(
            [gathered[:, :, :, b + j, :].reshape(256, LANES) for j in range(2)], axis=1
        )
        high, low = split(pair)
        stacked = jnp.concatenate([high, low, high], axis=0)
        both = jnp.dot(fx_t[...], stacked, preferred_element_type=jnp.float32)
        for owner in range(4):
            for j in range(2):
                x_out[owner, b + j] = both[owner * 32 : owner * 32 + 32, j * LANES : (j + 1) * LANES]
        for copy in x_pair(b):
            copy.start()
    for b in range(0, 8, 2):
        for copy in x_pair(b):
            copy.wait_recv()
        for j in (b, b + 1):
            core_out[:, j, :] = (x_out[x, j] + x_in[0, j]) + (x_in[1, j] + x_in[2, j])
    x_copies = [copy for b in range(0, 8, 2) for copy in x_pair(b)]

    for copy in (s_low, s_high, m_low, m_high, *fx_copies, *x_copies):
        copy.wait_send()

    def drain(k, carry):
        for copy in (
            *y_faces(faces_s, halo_s, fs_send, fs_recv, k),
            *y_faces(faces_m, halo_m, fm_send, fm_recv, k),
            *y_first(k), *y_second(k), *z_copies(k), core_copy(k),
        ):
            copy.wait_send()
        return carry

    lax.fori_loop(0, CHUNKS, drain, 0)


def on_device(scalar, prefactor, factor_x, factor_y, factor_z):
    f32, bf16 = jnp.float32, jnp.bfloat16
    dma = pltpu.SemaphoreType.DMA
    vmem = pltpu.VMEM
    padded = vmem((PLANES + 2, PARTS, PADDED, LANES), f32)
    faces = vmem((2, PLANES * PARTS, LANES), f32)
    anywhere = pl.BlockSpec(memory_space=pl.ANY)
    return pl.pallas_call(
        kernel,
        out_shape=(
            jax.ShapeDtypeStruct((PLANES, ROWS, PARTS * LANES), f32),
            jax.ShapeDtypeStruct((32, 8, LANES), f32),
        ),
        in_specs=[anywhere] * 5,
        out_specs=(pl.BlockSpec(memory_space=vmem), pl.BlockSpec(memory_space=vmem)),
        scratch_shapes=[
            padded, padded, vmem((PLANES, ROWS, PARTS * LANES), f32), vmem((2, PARTS, ROWS, LANES), f32), vmem((512, 512), bf16), vmem((CHUNK, ROWS, PARTS * LANES), bf16),
            vmem((512, 128), bf16), vmem((64, 64), f32), vmem((2, 2, 64, 512), f32),
            vmem((64, 192), bf16), vmem((128, 768), bf16),
            faces, faces, faces, faces,
            vmem((CHUNKS, 4, 2, CHUNK, 8, LANES), f32), vmem((CHUNKS, 2, 2, 2, 4, 8, LANES), f32),
            vmem((CHUNKS, 2, 2, 4, 8, LANES), f32), vmem((CHUNKS, 3, CHUNK, 8, LANES), f32),
            vmem((2, 2, PLANES, 8, LANES), f32), vmem((4, 8, 32, LANES), f32), vmem((3, 8, 32, LANES), f32),
            dma((CHUNKS, PARTS)), dma((CHUNKS,)), dma((3,)),
            dma((2, CHUNKS)), dma((2, CHUNKS)), dma((2, CHUNKS)), dma((2, CHUNKS)),
            dma((2,)), dma((2,)), dma((2,)), dma((2,)),
            dma((3,)), dma((3,)), dma((CHUNKS, 2)), dma((CHUNKS, 2)), dma((CHUNKS, 2)), dma((CHUNKS, 2)),
            dma((CHUNKS, 3)), dma((CHUNKS, 3)), dma((CHUNKS,)), dma((CHUNKS,)), dma((3, 4)), dma((3, 4)),
        ],
        compiler_params=pltpu.CompilerParams(collective_id=0, has_side_effects=True, vmem_limit_bytes=40 << 20),
        name="heun_tucker",
    )(scalar, prefactor, *(pltpu.with_memory_space_constraint(a, pltpu.HBM) for a in (factor_x, factor_y, factor_z)))


def solution(mesh):
    return jax.shard_map(
        on_device,
        mesh=mesh,
        in_specs=(P("gx", "gy", None), P("gx", "gy", None), P("gx", None), P("gy", None), P()),
        out_specs=(P("gx", "gy", None), P("gx", "gy", None)),
        check_vma=False,
    )
```

```python
import jax
import jax.numpy as jnp
from jax import lax
from jax.experimental import pallas as pl
from jax.experimental.pallas import tpu as pltpu
from jax.sharding import PartitionSpec as P

MESH = pl.DeviceIdType.MESH
spread_rate = 0.12
activation = 2.0
PLANES, ROWS, LANES, PARTS = 64, 64, 128, 4
CHUNK = 8
CHUNKS = PLANES // CHUNK
TOP = 8
PADDED = ROWS + 16
STRIP = CHUNK * PARTS
GROUP = 8
BAND = 16
FIX = 2
SECOND = 7
FIRST_SUM, SECOND_SUM, Z_SUM = SECOND + 2, SECOND + 4, SECOND + 6


def split(value):
    high = value.astype(jnp.bfloat16)
    low = (value - high.astype(jnp.float32)).astype(jnp.bfloat16)
    return high, low


def kernel(
    scalar, prefactor, factor_x, factor_y, factor_z, advanced, core_out,
    field, middle, pref, beside_x, band, lowered, fz, fy, fx_all, fy_t, fx_t,
    faces_s, halo_s, faces_m, halo_m,
    y_red, y_in1, y_in2, z_in, gathered, x_out, x_in,
    load_sem, pref_sem, small_sem,
    fs_send, fs_recv, fm_send, fm_recv, xs_send, xs_recv, xm_send, xm_recv,
    fx_send, fx_recv, y1_send, y1_recv, y2_send, y2_recv, z_send, z_recv, c_send, c_recv, xr_send, xr_recv,
):
    gx, gy = lax.axis_index("gx"), lax.axis_index("gy")
    core, x, zl = gx % 2, (gx // 2) % 4, gx // 8
    y, zh = gy % 4, gy // 4

    def device(core, x, zl, y, zh):
        return (zl * 8 + x * 2 + core, zh * 4 + y)

    up_x, down_x = ((gx + 1) % 16, gy), ((gx + 15) % 16, gy)
    up_y, down_y = (gx, (gy + 1) % 8), (gx, (gy + 7) % 8)
    y_by1 = y + 1 - 2 * (y % 2)
    y_by3 = 3 - y
    pair_a, pair_b = device(core, x, zl, y_by1, zh), device(core, x, zl, y_by3, zh)
    z_peers = [device(core, x, 1 - zl, y, zh), device(core, x, zl, y, 1 - zh), device(core, x, 1 - zl, y, 1 - zh)]
    partner = device(1 - core, x, zl, y, zh)
    fx_peers = [partner, z_peers[0], device(1 - core, x, 1 - zl, y, zh)]
    x_peers = [device(core, (x + j) % 4, zl, y, zh) for j in (1, 2, 3)]

    def load(k, part):
        return pltpu.make_async_copy(
            scalar.at[pl.ds(k * CHUNK, CHUNK), :, pl.ds(part * LANES, LANES)],
            field.at[pl.ds(k * CHUNK + 1, CHUNK), part, pl.ds(TOP, ROWS), :],
            load_sem.at[k, part],
        )

    def load_pref(k):
        rows = pl.ds(k * CHUNK, CHUNK)
        return pltpu.make_async_copy(prefactor.at[rows], pref.at[rows], pref_sem.at[k])

    for k in (7, 0, 6, 1, 2, 3, 4, 5):
        for part in range(PARTS):
            load(k, part).start()
    load_pref(7).start()
    load_pref(0).start()
    fx_load = pltpu.make_async_copy(factor_x, fx_all.at[core, zl], small_sem.at[0])
    fz_load = pltpu.make_async_copy(factor_z, fz, small_sem.at[1])
    fy_load = pltpu.make_async_copy(factor_y, fy, small_sem.at[2])
    fx_load.start()
    fz_load.start()
    fy_load.start()

    barrier = pltpu.get_barrier_semaphore()
    peers = [up_x, down_x, up_y, down_y, pair_a, pair_b, *z_peers, partner, fx_peers[2], *x_peers]
    for peer in peers:
        pl.semaphore_signal(barrier, inc=1, device_id=peer, device_id_type=MESH)

    def clear_plane(buffer, index):
        for part in range(PARTS):
            buffer[index, part, TOP : TOP + ROWS, :] = jnp.zeros((ROWS, LANES), jnp.float32)

    clear_plane(field, 0)
    clear_plane(field, PLANES + 1)

    def rows_of(buffer, k, row):
        start = (k * CHUNK + 1) * PARTS * PADDED + row
        return buffer.reshape((PLANES + 2) * PARTS * PADDED, LANES).at[pl.ds(start, STRIP, stride=PADDED), :]

    for k in range(CHUNKS):
        for row in (TOP - 1, TOP + ROWS):
            rows_of(field, k, row)[...] = jnp.zeros((STRIP, LANES), jnp.float32)
    along = lax.broadcasted_iota(jnp.int32, (512, 512), 0)
    across = lax.broadcasted_iota(jnp.int32, (512, 512), 1)
    band[...] = ((along == across + 1) | (across == along + 1)).astype(jnp.bfloat16)
    pl.semaphore_wait(barrier, len(peers))

    def remote(src, dst, send, recv, to):
        return pltpu.make_async_remote_copy(
            src_ref=src, dst_ref=dst, send_sem=send, recv_sem=recv, device_id=to, device_id_type=MESH
        )

    def plane_of(buffer, index):
        return buffer.at[index, :, pl.ds(TOP, ROWS), :]

    def y_faces(faces, halo, send, recv, k):
        rows = pl.ds(k * STRIP, STRIP)
        low = remote(faces.at[0, rows], halo.at[1, rows], send.at[0, k], recv.at[0, k], down_y)
        high = remote(faces.at[1, rows], halo.at[0, rows], send.at[1, k], recv.at[1, k], up_y)
        return low, high

    s_low = remote(plane_of(field, 1), beside_x.at[1], xs_send.at[0], xs_recv.at[0], down_x)
    s_high = remote(plane_of(field, PLANES), beside_x.at[0], xs_send.at[1], xs_recv.at[1], up_x)
    m_low = remote(plane_of(middle, 1), plane_of(middle, PLANES + 1), xm_send.at[0], xm_recv.at[0], down_x)
    m_high = remote(plane_of(middle, PLANES), plane_of(middle, 0), xm_send.at[1], xm_recv.at[1], up_x)

    def send_faces(k):
        for part in range(PARTS):
            load(k, part).wait()
        faces_s[0, pl.ds(k * STRIP, STRIP), :] = rows_of(field, k, TOP)[...]
        faces_s[1, pl.ds(k * STRIP, STRIP), :] = rows_of(field, k, TOP + ROWS - 1)[...]
        for copy in y_faces(faces_s, halo_s, fs_send, fs_recv, k):
            copy.start()

    send_faces(7)
    s_high.start()
    send_faces(0)
    s_low.start()

    def other_faces(k, carry):
        send_faces(k)
        return carry

    lax.fori_loop(1, CHUNKS - 1, other_faces, 0)

    fx_copies = [
        remote(fx_all.at[core, zl], fx_all.at[core, zl], fx_send.at[i], fx_recv.at[i], to)
        for i, to in enumerate(fx_peers)
    ]
    fx_load.wait()
    fz_load.wait()
    fy_load.wait()
    eye = (
        lax.broadcasted_iota(jnp.int32, (64, 64), 0) == lax.broadcasted_iota(jnp.int32, (64, 64), 1)
    ).astype(jnp.bfloat16)
    turned = (((1,), (1,)), ((), ()))
    fy_high, fy_low = (
        lax.dot_general(eye, part, turned, preferred_element_type=jnp.float32).astype(jnp.bfloat16)
        for part in split(fy[...])
    )
    fy_t[...] = jnp.concatenate([fy_high, fy_high, fy_low], axis=1)

    def beside_z(buffer, plane):
        planes = [
            jnp.concatenate([buffer[plane + i + 1, part, TOP : TOP + ROWS, :] for part in range(PARTS)], axis=1)
            for i in range(GROUP)
        ]
        return jnp.dot(
            jnp.concatenate(planes, axis=0).astype(jnp.bfloat16), band[...], preferred_element_type=jnp.float32
        )

    def stepped(buffer, plane, row, sums):
        at = plane + 1
        own = slice(TOP + row, TOP + row + BAND)
        centers = [buffer[at, part, own, :] for part in range(PARTS)]
        results = []
        for part, c in enumerate(centers):
            beside = buffer[at + 1, part, own, :] + buffer[at - 1, part, own, :]
            beside = beside + (
                buffer[at, part, TOP + row + 1 : TOP + row + 1 + BAND, :]
                + buffer[at, part, TOP + row - 1 : TOP + row - 1 + BAND, :]
            )
            beside = beside + sums[row : row + BAND, part * LANES : (part + 1) * LANES]
            factor = pref[plane, row : row + BAND, part * LANES : (part + 1) * LANES]
            source = factor * jnp.exp(-activation / (1.0 + c * c))
            results.append((1.0 - 6.0 * spread_rate) * c + spread_rate * beside + source)
        return results

    def first_stage(k):
        load_pref(k).wait()

        def group_step(g, carry):
            start = k * CHUNK + g * GROUP
            sums = beside_z(field, start)
            for i in range(GROUP):
                plane = start + i
                for row in range(0, ROWS, BAND):
                    for part, value in enumerate(stepped(field, plane, row, sums[i * ROWS : (i + 1) * ROWS])):
                        middle[plane + 1, part, TOP + row : TOP + row + BAND, :] = value
            return carry

        lax.fori_loop(0, CHUNK // GROUP, group_step, 0)

    def add_x(plane, side, inside):
        for part in range(PARTS):
            own = (plane + 1, part, slice(TOP, TOP + ROWS), slice(None))
            middle[own] = middle[own] + spread_rate * jnp.where(inside, beside_x[side, part], 0.0)

    def add_halo(k):
        @pl.when(k == CHUNKS - 1)
        def _():
            s_low.wait_recv()
            add_x(PLANES - 1, 1, gx < 15)

        @pl.when(k == 0)
        def _():
            s_high.wait_recv()
            add_x(0, 0, gx > 0)

        for copy in y_faces(faces_s, halo_s, fs_send, fs_recv, k):
            copy.wait_recv()
        rows = pl.ds(k * STRIP, STRIP)
        for side, inside, row in ((0, gy > 0, TOP), (1, gy < 7, TOP + ROWS - 1)):
            edge = rows_of(middle, k, row)
            value = edge[...] + spread_rate * jnp.where(inside, halo_s[side, rows, :], 0.0)
            faces_m[side, rows, :] = value
            edge[...] = value
        for copy in y_faces(faces_m, halo_m, fm_send, fm_recv, k):
            copy.start()

        @pl.when(k == CHUNKS - 1)
        def _():
            m_high.start()

        @pl.when(k == 0)
        def _():
            m_low.start()

    def y_first(k):
        a = remote(y_red.at[k, pl.ds(1, 2), :, pl.ds(0, 4)], y_in1.at[k, 0], y1_send.at[k, 0], y1_recv.at[k, 0], pair_a)
        b = remote(y_red.at[k, pl.ds(2, 2), :, pl.ds(4, 4)], y_in1.at[k, 1], y1_send.at[k, 1], y1_recv.at[k, 1], pair_b)
        return a, b

    def y_second(k):
        a = remote(y_red.at[k, 3, :, pl.ds(0, 4)], y_in2.at[k, 0], y2_send.at[k, 0], y2_recv.at[k, 0], pair_b)
        b = remote(y_red.at[k, 1, :, pl.ds(4, 4)], y_in2.at[k, 1], y2_send.at[k, 1], y2_recv.at[k, 1], pair_a)
        return a, b

    def z_copies(k):
        return [
            remote(y_red.at[k, 0, block], z_in.at[k, i], z_send.at[k, i], z_recv.at[k, i], z_peers[i])
            for i, block in enumerate((zh, 1 - zh, 1 - zh))
        ]

    def core_copy(k):
        block = gathered.at[core, :, pl.ds(k * CHUNK, CHUNK)]
        return remote(block, block, c_send.at[k], c_recv.at[k], partner)

    def second_stage(k):
        low, high = y_faces(faces_m, halo_m, fm_send, fm_recv, k)
        low.wait_recv()
        high.wait_recv()

        @pl.when(k == CHUNKS - 1)
        def _():
            m_low.wait_recv()

            @pl.when(gx == 15)
            def _():
                clear_plane(middle, PLANES + 1)

        @pl.when(k == 0)
        def _():
            m_high.wait_recv()

            @pl.when(gx == 0)
            def _():
                clear_plane(middle, 0)

        rows = pl.ds(k * STRIP, STRIP)
        rows_of(middle, k, TOP - 1)[...] = jnp.where(gy > 0, halo_m[0, rows, :], 0.0)
        rows_of(middle, k, TOP + ROWS)[...] = jnp.where(gy < 7, halo_m[1, rows, :], 0.0)

        def group_step(g, carry):
            start = k * CHUNK + g * GROUP
            sums = beside_z(middle, start)
            for i in range(GROUP):
                plane = start + i
                for row in range(0, ROWS, BAND):
                    for part, value in enumerate(stepped(middle, plane, row, sums[i * ROWS : (i + 1) * ROWS])):
                        value = 0.5 * (field[plane + 1, part, TOP + row : TOP + row + BAND, :] + value)
                        lanes = slice(part * LANES, (part + 1) * LANES)
                        advanced[plane, row : row + BAND, lanes] = value
                        lowered[g * GROUP + i, row : row + BAND, lanes] = value.astype(jnp.bfloat16)
            return carry

        lax.fori_loop(0, CHUNK // GROUP, group_step, 0)
        z_red = jnp.dot(
            lowered[...].reshape(CHUNK * ROWS, PARTS * LANES), fz[...], preferred_element_type=jnp.float32
        )
        blocks = [y, y_by1, (y + 2) % 4, y_by3]
        planes = jnp.concatenate([z_red[i * ROWS : (i + 1) * ROWS] for i in range(CHUNK)], axis=1)
        high, low = split(planes)
        both = jnp.dot(
            fy_t[...], jnp.concatenate([high, low, high], axis=0), preferred_element_type=jnp.float32
        )
        for owner in range(8):
            for i in range(CHUNK):
                y_red[k, blocks[owner % 4], owner // 4, i] = both[
                    owner * 8 : owner * 8 + 8, i * LANES : (i + 1) * LANES
                ]
        for copy in y_first(k):
            copy.start()

    def y_first_done(k):
        for copy in y_first(k):
            copy.wait_recv()
        y_red[k, 0, :, 0:4] += y_in1[k, 0, 0]
        y_red[k, 3, :, 0:4] += y_in1[k, 0, 1]
        y_red[k, 1, :, 4:8] += y_in1[k, 1, 0]
        y_red[k, 0, :, 4:8] += y_in1[k, 1, 1]
        for copy in y_second(k):
            copy.start()

    def y_second_done(k):
        for copy in y_second(k):
            copy.wait_recv()
        y_red[k, 0, :, 0:4] += y_in2[k, 0]
        y_red[k, 0, :, 4:8] += y_in2[k, 1]
        for copy in z_copies(k):
            copy.start()

    def z_done(k):
        for copy in z_copies(k):
            copy.wait_recv()
        rows = pl.ds(k * CHUNK, CHUNK)
        gathered[core, zl, rows] = y_red[k, 0, zh] + z_in[k, 1]
        gathered[core, 1 - zl, rows] = z_in[k, 0] + z_in[k, 2]
        core_copy(k).start()

    def prepare_x():
        for copy in fx_copies:
            copy.wait_recv()
        entry = lax.broadcasted_iota(jnp.int32, (128, 512), 0)
        wanted = zl * 256 + (entry // 32) * 64 + core * 32 + entry % 32
        picked = (lax.broadcasted_iota(jnp.int32, (128, 512), 1) == wanted).astype(jnp.bfloat16)
        high, low = (
            lax.dot_general(picked, part, turned, preferred_element_type=jnp.float32).astype(jnp.bfloat16)
            for part in split(fx_all[...].reshape(256, 512))
        )
        fx_t[...] = jnp.concatenate([high, high, low], axis=1)

    def step(t, carry):
        pl.when(t < CHUNKS - 2)(lambda: load_pref(t + 1).start())

        @pl.when(t == 3)
        def _():
            for copy in fx_copies:
                copy.start()

        pl.when(t < CHUNKS)(lambda: first_stage((t + CHUNKS - 1) % CHUNKS))
        pl.when((t >= FIX) & (t < CHUNKS + FIX))(lambda: add_halo((t - FIX + CHUNKS - 1) % CHUNKS))
        pl.when((t >= SECOND) & (t < CHUNKS + SECOND))(lambda: second_stage(t - SECOND))
        pl.when((t >= FIRST_SUM) & (t < CHUNKS + FIRST_SUM))(lambda: y_first_done(t - FIRST_SUM))
        pl.when(t == CHUNKS + FIRST_SUM - 1)(prepare_x)
        pl.when((t >= SECOND_SUM) & (t < CHUNKS + SECOND_SUM))(lambda: y_second_done(t - SECOND_SUM))
        pl.when(t >= Z_SUM)(lambda: z_done(t - Z_SUM))
        return carry

    lax.fori_loop(0, CHUNKS + Z_SUM, step, 0)

    def x_pair(b):
        rows = pl.ds(b, 2)
        return [
            remote(
                x_out.at[(x + 1 + i) % 4, rows], x_in.at[i, rows], xr_send.at[i, b // 2], xr_recv.at[i, b // 2], to
            )
            for i, to in enumerate(x_peers)
        ]

    for k in range(CHUNKS):
        core_copy(k).wait_recv()
    for b in range(0, 8, 2):
        pair = jnp.concatenate(
            [gathered[:, :, :, b + j, :].reshape(256, LANES) for j in range(2)], axis=1
        )
        high, low = split(pair)
        stacked = jnp.concatenate([high, low, high], axis=0)
        both = jnp.dot(fx_t[...], stacked, preferred_element_type=jnp.float32)
        for owner in range(4):
            for j in range(2):
                x_out[owner, b + j] = both[owner * 32 : owner * 32 + 32, j * LANES : (j + 1) * LANES]
        for copy in x_pair(b):
            copy.start()
    for b in range(0, 8, 2):
        for copy in x_pair(b):
            copy.wait_recv()
        for j in (b, b + 1):
            core_out[:, j, :] = (x_out[x, j] + x_in[0, j]) + (x_in[1, j] + x_in[2, j])
    x_copies = [copy for b in range(0, 8, 2) for copy in x_pair(b)]

    for copy in (s_low, s_high, m_low, m_high, *fx_copies, *x_copies):
        copy.wait_send()

    def drain(k, carry):
        for copy in (
            *y_faces(faces_s, halo_s, fs_send, fs_recv, k),
            *y_faces(faces_m, halo_m, fm_send, fm_recv, k),
            *y_first(k), *y_second(k), *z_copies(k), core_copy(k),
        ):
            copy.wait_send()
        return carry

    lax.fori_loop(0, CHUNKS, drain, 0)


def on_device(scalar, prefactor, factor_x, factor_y, factor_z):
    f32, bf16 = jnp.float32, jnp.bfloat16
    dma = pltpu.SemaphoreType.DMA
    vmem = pltpu.VMEM
    padded = vmem((PLANES + 2, PARTS, PADDED, LANES), f32)
    faces = vmem((2, PLANES * PARTS, LANES), f32)
    anywhere = pl.BlockSpec(memory_space=pl.ANY)
    return pl.pallas_call(
        kernel,
        out_shape=(
            jax.ShapeDtypeStruct((PLANES, ROWS, PARTS * LANES), f32),
            jax.ShapeDtypeStruct((32, 8, LANES), f32),
        ),
        in_specs=[anywhere] * 5,
        out_specs=(pl.BlockSpec(memory_space=vmem), pl.BlockSpec(memory_space=vmem)),
        scratch_shapes=[
            padded, padded, vmem((PLANES, ROWS, PARTS * LANES), f32), vmem((2, PARTS, ROWS, LANES), f32), vmem((512, 512), bf16), vmem((CHUNK, ROWS, PARTS * LANES), bf16),
            vmem((512, 128), bf16), vmem((64, 64), f32), vmem((2, 2, 64, 512), f32),
            vmem((64, 192), bf16), vmem((128, 768), bf16),
            faces, faces, faces, faces,
            vmem((CHUNKS, 4, 2, CHUNK, 8, LANES), f32), vmem((CHUNKS, 2, 2, 2, 4, 8, LANES), f32),
            vmem((CHUNKS, 2, 2, 4, 8, LANES), f32), vmem((CHUNKS, 3, CHUNK, 8, LANES), f32),
            vmem((2, 2, PLANES, 8, LANES), f32), vmem((4, 8, 32, LANES), f32), vmem((3, 8, 32, LANES), f32),
            dma((CHUNKS, PARTS)), dma((CHUNKS,)), dma((3,)),
            dma((2, CHUNKS)), dma((2, CHUNKS)), dma((2, CHUNKS)), dma((2, CHUNKS)),
            dma((2,)), dma((2,)), dma((2,)), dma((2,)),
            dma((3,)), dma((3,)), dma((CHUNKS, 2)), dma((CHUNKS, 2)), dma((CHUNKS, 2)), dma((CHUNKS, 2)),
            dma((CHUNKS, 3)), dma((CHUNKS, 3)), dma((CHUNKS,)), dma((CHUNKS,)), dma((3, 4)), dma((3, 4)),
        ],
        compiler_params=pltpu.CompilerParams(collective_id=0, has_side_effects=True, vmem_limit_bytes=40 << 20),
        name="heun_tucker",
    )(scalar, prefactor, *(pltpu.with_memory_space_constraint(a, pltpu.HBM) for a in (factor_x, factor_y, factor_z)))


def solution(mesh):
    return jax.shard_map(
        on_device,
        mesh=mesh,
        in_specs=(P("gx", "gy", None), P("gx", "gy", None), P("gx", None), P("gy", None), P()),
        out_specs=(P("gx", "gy", None), P("gx", "gy", None)),
        check_vma=False,
    )
```
